32 devices in a mesh: groups: 2 (over x), col: 16 (over z, y, core).
Axes of the slice: x: 2, y: 2, z: 4, core: 2. Of those that a mesh axis runs over, the one named last changes fastest.
Arguments:
- features: bfloat16 [32, 8, 8192], P(('groups', 'col')), parts along dimension 0
- zone_ids: int32 [32], P(('groups', 'col')), parts along dimension 0, may hold values from 0 to 7, as said below
- golden_owner: int32 [16], P('groups'), parts along dimension 0, may hold values from 0 to 15, as said below
- defect_mask: int32 [32, 8, 128], P(('groups', 'col')), parts along dimension 0, may hold values 0 or 1
- kernels: bfloat16 [2, 576, 64], replicated, may hold values from -0.25 to 0.25
Outputs:
- score: float32 [32, 8, 128], P(('groups', 'col')), parts along dimension 0
The draws below stay inside these ranges and needn't reach their ends.
There are 2 independent parts, one for each index of `groups`. The reference program is written for one: setup_inputs(seed, part) draws one part's arguments, and reference() takes and returns one part's arrays. A program takes and returns all parts, laid end to end along the dimension named above; an argument that names none is the same for every part. Nothing has to cross between parts.
Inputs may be any that keep to these rules, and one draw needn't show every extreme that they name: `zone_ids`: every zone holds at least one die. golden_owner[z] is a die of zone z.
All inputs are finite; a program needn't handle non-finite values. No bound on the sum of `defect_mask` on one device may be relied on, other than what follows from the above.
Results may differ from the reference program's by a relative error of at most 0.0039.
Values may be sent and summed in bfloat16 or wider, within the bound.
A program may use at most 64 MiB of HBM per device.

```python
import jax
import jax.numpy as jnp
from jax import lax

C = 64
H = 8
W = 128
SHIFT = 6
BOX = 5
Z = 8
DIES = 16


def layout(key):
    base = jax.random.fold_in(key, 101)
    key_order = jax.random.fold_in(base, 1)
    key_map = jax.random.fold_in(base, 2)
    key_pick = jax.random.fold_in(base, 3)
    order = jax.random.permutation(key_order, DIES).astype(jnp.int32)
    zone_map = jax.random.permutation(key_map, Z).astype(jnp.int32)
    picks = jax.random.randint(key_pick, (3, DIES), 0, Z)
    common = zone_map[jnp.min(picks, axis=0)]
    slots = jnp.arange(DIES, dtype=jnp.int32)
    assign = jnp.where(slots < Z, slots, common).astype(jnp.int32)
    zones = jnp.zeros((DIES,), jnp.int32).at[order].set(assign)
    owners = order[0:Z]
    return (zones, owners)


def draw_zone_ids(key, part):
    zones, owners = layout(key)
    return zones


def draw_golden_owner(key, part):
    zones, owners = layout(key)
    return owners


def draw_features(key, part):
    zones, owners = layout(key)
    base = jax.random.fold_in(key, 202)
    key_rough = jax.random.fold_in(base, 1)
    key_noise = jax.random.fold_in(base, 2)
    key_rank = jax.random.fold_in(base, 3)
    key_spot = jax.random.fold_in(base, 4)
    key_size = jax.random.fold_in(base, 5)
    key_sign = jax.random.fold_in(base, 7)
    key_magn = jax.random.fold_in(base, 8)
    side = 2 * SHIFT + 1
    others = min(side, 2 * H - 1) * min(side, 2 * W - 1) - 1
    rank = jax.random.permutation(key_rank, Z).astype(jnp.float32)
    share = 0.24 + 0.09 * rank / (Z - 1)
    rough_scale = jnp.sqrt(share / (1.0 - share))
    leak = 1.2 * others * jnp.exp(-32.0 * share)
    amplify = 1.0 / (leak * rough_scale)
    signs = jnp.where(jax.random.bernoulli(key_sign, 0.5, (Z, C)), 1.0, -1.0).astype(jnp.float32)
    magnitude = jax.random.uniform(key_magn, (Z, C), jnp.float32, 0.8, 1.2)
    rough = jax.random.normal(key_rough, (Z, H, W, C), jnp.float32)
    noise = jax.random.normal(key_noise, (DIES, H, W, C), jnp.float32)
    zone_scale = jnp.ones((Z,), jnp.float32)
    pattern = (signs * magnitude)[:, None, None, :] + rough_scale[:, None, None, None] * rough
    pattern = pattern * amplify[:, None, None, None]
    tiles = jnp.take(pattern, zones, axis=0)
    spots = (jax.random.uniform(key_spot, (DIES, H, W, 1)) < 0.02).astype(jnp.float32)
    spots = 4.0 * spots * jax.random.normal(key_size, (DIES, H, W, C), jnp.float32)
    whole = (tiles + noise + spots) * jnp.take(zone_scale, zones)[:, None, None, None]
    return whole.reshape(DIES, H, W * C).astype(jnp.bfloat16)


def with_ends(values, stream_key, smallest, high):
    spot = [jax.random.randint(jax.random.fold_in(stream_key, axis), (), 0, length) for axis, length in enumerate(values.shape)]
    widest = values.shape.index(max(values.shape))
    next_to = spot[:widest] + [(spot[widest] + 1) % values.shape[widest]] + spot[widest + 1:]
    return values.at[tuple(spot)].set(smallest).at[tuple(next_to)].set(high)


def scatter_about(key, shape, deviation, limit, kind=jnp.bfloat16):
    return jnp.clip(deviation * jax.random.normal(key, shape, jnp.float32), -limit, limit).astype(kind)


def setup_inputs(seed: int = 0, part: int = 0) -> dict:
    keys = jax.random.split(jax.random.key(seed), 6)
    part_splits = jax.random.split(jax.random.fold_in(keys[5], part), 6)
    return {
        "features": draw_features(jax.random.fold_in(jax.random.fold_in(keys[5], part), 71), part),
        "zone_ids": draw_zone_ids(jax.random.fold_in(jax.random.fold_in(keys[5], part), 71), part),
        "golden_owner": draw_golden_owner(jax.random.fold_in(jax.random.fold_in(keys[5], part), 71), part),
        "defect_mask": with_ends((jax.random.randint(part_splits[3], (DIES, H, W), 0, 2) < 1).astype(jnp.int32), jax.random.fold_in(part_splits[3], 1), 0, 1),
        "kernels": scatter_about(keys[4], (2, 9 * C, C), (9 * C) ** -0.5, 0.25),
    }


def box_sum(plane):
    rows = plane.shape[0]
    cols = plane.shape[1]
    reach = BOX // 2
    padded = jnp.pad(plane, ((reach, reach), (reach, reach)))
    across = padded[0:rows]
    for offset in range(1, BOX):
        across = across + padded[offset:offset + rows]
    total = across[:, 0:cols]
    for offset in range(1, BOX):
        total = total + across[:, offset:offset + cols]
    return total

def align_golden(test_tile, golden_tile):
    height, width, chans = test_tile.shape
    side = 2 * SHIFT + 1
    test_f = test_tile.astype(jnp.float32)
    padded = jnp.pad(golden_tile.astype(jnp.float32), ((SHIFT, SHIFT), (SHIFT, SHIFT), (0, 0)))
    self_energy = box_sum(lax.optimization_barrier(jnp.sum(test_f * test_f, axis=-1)))

    def shifted(index):
        row_off = (index // side).astype(jnp.int32)
        col_off = (index % side).astype(jnp.int32)
        return lax.dynamic_slice(padded, (row_off, col_off, jnp.int32(0)), (height, width, chans))

    def logit(index):
        moved = shifted(index)
        cross = box_sum(lax.optimization_barrier(jnp.sum(test_f * moved, axis=-1)))
        other = box_sum(lax.optimization_barrier(jnp.sum(moved * moved, axis=-1)))
        return 32.0 * cross / jnp.sqrt(self_energy * other + 1e-05)
    shift_ids = jnp.arange(side * side, dtype=jnp.int32)
    logits = lax.map(logit, shift_ids)
    expo = jnp.exp(logits)
    weights = expo / lax.optimization_barrier(jnp.sum(expo, axis=0))

    def accumulate(total, pair):
        index, weight = pair
        return (total + weight[:, :, None] * shifted(index), None)
    aligned, _ = lax.scan(accumulate, jnp.zeros((height, width, chans), jnp.float32), (shift_ids, weights))
    return aligned

def conv_three(tile, kernel):
    height, width, chans = tile.shape
    padded = jnp.pad(tile, ((1, 1), (1, 1), (0, 0)))
    total = jnp.zeros((height * width, kernel.shape[1]), jnp.float32)
    for tap in range(9):
        row_off = tap // 3
        col_off = tap % 3
        window = padded[row_off:row_off + height, col_off:col_off + width].reshape(height * width, chans)
        total = total + jnp.dot(window, kernel[tap * chans:(tap + 1) * chans], preferred_element_type=jnp.float32)
    return total.reshape(height, width, kernel.shape[1])

def inspect_die(test_tile, golden_tile, kernels):
    aligned = align_golden(test_tile, golden_tile)
    residual = (test_tile.astype(jnp.float32) - aligned).astype(jnp.bfloat16)
    hidden = jax.nn.relu(conv_three(residual, kernels[0])).astype(jnp.bfloat16)
    refined = residual.astype(jnp.float32) + conv_three(hidden, kernels[1])
    return lax.optimization_barrier(jnp.mean(refined * refined, axis=-1))

def reference(features, zone_ids, golden_owner, defect_mask, kernels):

    def one_die(die):
        test_tile = features[die].reshape(H, W, C)
        golden_tile = features[golden_owner[zone_ids[die]]].reshape(H, W, C)
        return inspect_die(test_tile, golden_tile, kernels)
    energy = lax.map(one_die, jnp.arange(DIES, dtype=jnp.int32))
    masked = defect_mask.astype(jnp.float32)
    die_sum = lax.optimization_barrier(jnp.sum(energy * masked, axis=(1, 2)))
    die_count = lax.optimization_barrier(jnp.sum(masked, axis=(1, 2)))
    onehot = (zone_ids[:, None] == jnp.arange(Z, dtype=jnp.int32)[None, :]).astype(jnp.float32)
    zone_sum = lax.optimization_barrier(jnp.sum(onehot * die_sum[:, None], axis=0))
    zone_count = lax.optimization_barrier(jnp.sum(onehot * die_count[:, None], axis=0))
    zone_mean = zone_sum / jnp.maximum(zone_count, 1.0)
    mine = lax.optimization_barrier(jnp.sum(onehot * zone_mean[None, :], axis=1))
    return energy / (mine[:, None, None] + 0.01)
```

```python
import functools

import jax
import jax.numpy as jnp
from jax import lax
from jax.experimental import pallas as pl
from jax.experimental.pallas import tpu as pltpu
from jax.sharding import PartitionSpec as P

C = 64
H = 8
W = 128
SHIFT = 6
REACH = 2
Z = 8
MESH = pl.DeviceIdType.MESH


def gather_kernel(n, nz, ny, zone_ref, owner_ref, t_ref, g_ref, slots, own_sem, recv, sends):
    me = lax.axis_index("col")
    core = lax.rem(me, 2)
    yy = lax.rem(me // 2, ny)
    zz = me // (2 * ny)

    def idx(z, y, c):
        return (z * ny + y) * 2 + c

    up = idx(zz + 1, yy, core)
    down = idx(zz - 1, yy, core)
    side = idx(zz, 1 - yy, core)
    mate = idx(zz, yy, 1 - core)
    has_up = zz + 1 < nz
    has_down = zz > 0

    barrier = pltpu.get_barrier_semaphore()

    def greet(dev):
        pl.semaphore_signal(barrier, inc=1, device_id={"col": dev}, device_id_type=MESH)

    @pl.when(has_up)
    def _():
        greet(up)

    @pl.when(has_down)
    def _():
        greet(down)

    if ny == 2:
        greet(side)
    greet(mate)
    peers = ny + jnp.where(has_up, 1, 0) + jnp.where(has_down, 1, 0)
    pl.semaphore_wait(barrier, peers)

    def copy(kind, slot, dev, src=None):
        return pltpu.make_async_remote_copy(
            src_ref=slots.at[slot] if src is None else src,
            dst_ref=slots.at[slot],
            send_sem=sends.at[kind, slot],
            recv_sem=recv.at[slot],
            device_id={"col": dev},
            device_id_type=MESH,
        )

    def arrive(slot):
        copy(0, slot, mate).wait_recv()

    @pl.when(has_up)
    def _():
        copy(0, me, up, t_ref).start()

    @pl.when(has_down)
    def _():
        copy(1, me, down, t_ref).start()

    if ny == 2:
        copy(2, me, side, t_ref).start()
    copy(3, me, mate, t_ref).start()
    own = pltpu.make_async_copy(t_ref, slots.at[me], own_sem)
    own.start()

    def from_side(z):
        slot = idx(z, 1 - yy, core)
        arrive(slot)
        copy(3, slot, mate).start()

    for s in range(1, nz):
        below = zz - s
        above = zz + s

        @pl.when(below >= 0)
        def _():
            slot = idx(below, yy, core)
            arrive(slot)

            @pl.when(has_up)
            def _():
                copy(0, slot, up).start()

            if ny == 2:
                copy(2, slot, side).start()
            copy(3, slot, mate).start()

        @pl.when(above < nz)
        def _():
            slot = idx(above, yy, core)
            arrive(slot)

            @pl.when(has_down)
            def _():
                copy(1, slot, down).start()

            if ny == 2:
                copy(2, slot, side).start()
            copy(3, slot, mate).start()

        if ny == 2:
            if s == 1:
                from_side(zz)
            else:

                @pl.when(zz - (s - 1) >= 0)
                def _():
                    from_side(zz - (s - 1))

                @pl.when(zz + (s - 1) < nz)
                def _():
                    from_side(zz + (s - 1))

    if ny == 2:

        @pl.when(zz - (nz - 1) >= 0)
        def _():
            from_side(zz - (nz - 1))

        @pl.when(zz + (nz - 1) < nz)
        def _():
            from_side(zz + (nz - 1))

    for z in range(nz):
        for y in range(ny):
            arrive(idx(z, y, 1 - core))
    own.wait()

    def sent(kind, slot):
        copy(kind, slot, mate).wait_send()

    for z in range(nz):
        slot = idx(z, yy, core)

        @pl.when(jnp.logical_and(has_up, z <= zz))
        def _():
            sent(0, slot)

        @pl.when(jnp.logical_and(has_down, z >= zz))
        def _():
            sent(1, slot)

        if ny == 2:
            sent(2, slot)
        for y in range(ny):
            sent(3, idx(z, y, core))

    g_ref[...] = slots[owner_ref[zone_ref[0]]]


def gather_golden(zone, owners, tile, n):
    ny = 2 if n == 16 else 1
    nz = n // (2 * ny)
    return pl.pallas_call(
        functools.partial(gather_kernel, n, nz, ny),
        out_shape=jax.ShapeDtypeStruct(tile.shape, tile.dtype),
        in_specs=[
            pl.BlockSpec(memory_space=pltpu.SMEM),
            pl.BlockSpec(memory_space=pltpu.SMEM),
            pl.BlockSpec(memory_space=pltpu.VMEM),
        ],
        out_specs=pl.BlockSpec(memory_space=pltpu.VMEM),
        scratch_shapes=[
            pltpu.VMEM((n,) + tile.shape, tile.dtype),
            pltpu.SemaphoreType.DMA,
            pltpu.SemaphoreType.DMA((n,)),
            pltpu.SemaphoreType.DMA((4, n)),
        ],
        compiler_params=pltpu.CompilerParams(collective_id=0, has_side_effects=True),
    )(zone, owners, tile)


def lane_box(v):
    lane = lax.broadcasted_iota(jnp.int32, v.shape, v.ndim - 1)
    total = v
    for d in range(1, REACH + 1):
        right = pltpu.roll(v, d, v.ndim - 1)
        left = pltpu.roll(v, W - d, v.ndim - 1)
        total = total + jnp.where(lane >= d, right, 0.0) + jnp.where(lane < W - d, left, 0.0)
    return total


def rotate_rows(v, bits, sign):
    for k in range(4):
        step = 1 << k
        moved = pltpu.roll(v, (16 - step) if sign < 0 else step, v.ndim - 2)
        v = jnp.where(bits[k], moved, v)
    return v


def conv_taps(tile_f, stack, weights):
    lane = lax.rem(lax.broadcasted_iota(jnp.int32, (C, H * W), 1), W)
    pixels = H * W
    left = jnp.where(lane >= 1, pltpu.roll(tile_f, 1, 1), 0.0).astype(jnp.bfloat16)
    right = jnp.where(lane < W - 1, pltpu.roll(tile_f, pixels - 1, 1), 0.0).astype(jnp.bfloat16)
    views = (left, tile_f.astype(jnp.bfloat16), right)
    zeros = jnp.zeros((C, W), jnp.bfloat16)
    for tap in range(9):
        dy = tap // 3 - 1
        v = views[tap % 3]
        rows = slice(tap * C, (tap + 1) * C)
        if dy == 0:
            stack[rows, :] = v
        elif dy < 0:
            stack[rows, 0:W] = zeros
            stack[rows, W:pixels] = v[:, 0 : pixels - W]
        else:
            stack[rows, 0 : pixels - W] = v[:, W:pixels]
            stack[rows, pixels - W : pixels] = zeros
    return jnp.dot(weights, stack[...], preferred_element_type=jnp.float32)


def inspect_kernel(zone_ref, t_ref, g_ref, mask_ref, k_ref, energy_ref, part_ref, cross, res, stack):
    gt = g_ref[...]
    g_f = gt.astype(jnp.float32).T
    g = g_f.astype(jnp.bfloat16)

    fold_row = lax.broadcasted_iota(jnp.int32, (8, 16, W), 0) * 16 + lax.broadcasted_iota(
        jnp.int32, (8, 16, W), 1
    )
    gap = fold_row - lax.broadcasted_iota(jnp.int32, (8, 16, W), 2)
    near = jnp.logical_and(gap >= -8, gap < 8)
    near_f = jnp.where(near, 1.0, 0.0)
    near_b = near_f.astype(jnp.bfloat16)

    def bits_of(shape):
        spin = lax.broadcasted_iota(jnp.int32, shape, len(shape) - 1) + 8
        return [((spin >> k) & 1) == 1 for k in range(4)]

    bits3 = bits_of((H, 16, W))

    def band(full):
        v = full.reshape(H, 8, 16, W)
        v = jnp.sum(v * near_f[None], axis=1)
        return lane_box(rotate_rows(v, bits3, -1))

    for y in range(H):
        gram = jnp.dot(g, t_ref[:, y * W : (y + 1) * W], preferred_element_type=jnp.float32)
        cross[y] = band(gram)
    square = jnp.sum(g_f * g_f, axis=1, keepdims=True)
    other_rows = band(jnp.broadcast_to(square, (H * W, W)))
    others = [other_rows[r] for r in range(H)]

    t_f = t_ref[...].astype(jnp.float32)
    own = jnp.sum(t_f * t_f, axis=0, keepdims=True)
    own_rows = [own[:, y * W : (y + 1) * W] for y in range(H)]
    row_id = lax.broadcasted_iota(jnp.int32, (16, W), 0)
    used = jnp.logical_and(row_id >= 8 - SHIFT, row_id <= 8 + SHIFT)

    for y in range(H):
        lo_y, hi_y = max(0, y - REACH), min(H - 1, y + REACH)
        self_energy = own_rows[lo_y]
        for r in range(lo_y + 1, hi_y + 1):
            self_energy = self_energy + own_rows[r]
        self_energy = jnp.broadcast_to(lane_box(self_energy), (16, W))
        denom = jnp.zeros((16, W), jnp.float32)
        picked = {}
        for a in range(-SHIFT, SHIFT + 1):
            num = None
            oth = None
            for r in range(lo_y, hi_y + 1):
                if 0 <= r + a < H:
                    num = cross[r, r + a] if num is None else num + cross[r, r + a]
                    oth = others[r + a] if oth is None else oth + others[r + a]
            if num is None:
                expo = jnp.where(used, 1.0, 0.0)
            else:
                logit = (32.0 * num) * lax.rsqrt(self_energy * oth + 1e-05)
                expo = jnp.where(used, jnp.exp(logit), 0.0)
            denom = denom + expo
            if 0 <= y + a < H:
                picked[y + a] = expo
        stacked = jnp.stack(
            [picked[r] if r in picked else jnp.zeros((16, W), jnp.float32) for r in range(H)]
        )
        stacked = rotate_rows(stacked, bits3, 1)
        high = stacked.astype(jnp.bfloat16)
        low = (stacked - high.astype(jnp.float32)).astype(jnp.bfloat16)
        wide_high = (high[:, None] * near_b[None]).reshape(H * W, W)
        wide_low = (low[:, None] * near_b[None]).reshape(H * W, W)
        numer = jnp.dot(gt, wide_high, preferred_element_type=jnp.float32) + jnp.dot(
            gt, wide_low, preferred_element_type=jnp.float32
        )
        total = jnp.sum(denom, axis=0, keepdims=True)
        aligned = numer / total
        cols = slice(y * W, (y + 1) * W)
        res[:, cols] = (t_f[:, cols] - aligned).astype(jnp.bfloat16).astype(jnp.float32)

    residual = res[...]
    hidden = jnp.maximum(conv_taps(residual, stack, k_ref[0]), 0.0)
    hidden = hidden.astype(jnp.bfloat16).astype(jnp.float32)
    refined = residual + conv_taps(hidden, stack, k_ref[1])
    flat = jnp.sum(refined * refined, axis=0, keepdims=True) * (1.0 / C)
    energy = jnp.concatenate([flat[:, y * W : (y + 1) * W] for y in range(H)], axis=0)
    energy_ref[...] = energy
    masked = mask_ref[...].astype(jnp.float32)
    die_sum = jnp.sum(jnp.sum(energy * masked, axis=1, keepdims=True), axis=0, keepdims=True)
    die_count = jnp.sum(jnp.sum(masked, axis=1, keepdims=True), axis=0, keepdims=True)
    row8 = lax.broadcasted_iota(jnp.int32, (H, W), 0)
    lane8 = lax.broadcasted_iota(jnp.int32, (H, W), 1)
    pair = jnp.where(row8 == 0, die_sum, die_count)
    part_ref[...] = jnp.where(lane8 == zone_ref[0], pair, 0.0)


def inspect(zone, tile, golden, mask, kernels_t):
    vmem = pl.BlockSpec(memory_space=pltpu.VMEM)
    plane = jax.ShapeDtypeStruct((H, W), jnp.float32)
    return pl.pallas_call(
        inspect_kernel,
        out_shape=(plane, plane),
        in_specs=[pl.BlockSpec(memory_space=pltpu.SMEM), vmem, vmem, vmem, vmem],
        out_specs=(vmem, vmem),
        scratch_shapes=[
            pltpu.VMEM((H, H, 16, W), jnp.float32),
            pltpu.VMEM((C, H * W), jnp.float32),
            pltpu.VMEM((9 * C, H * W), jnp.bfloat16),
        ],
    )(zone, tile, golden, mask, kernels_t)


def score_kernel(n, zone_ref, energy_ref, part_ref, score_ref, parts, send, recv):
    me = lax.axis_index("col")
    barrier = pltpu.get_barrier_semaphore()
    for k in range(1, n):
        pl.semaphore_signal(
            barrier, inc=1, device_id={"col": lax.rem(me + k, n)}, device_id_type=MESH
        )
    pl.semaphore_wait(barrier, n - 1)

    def copy(k):
        return pltpu.make_async_remote_copy(
            src_ref=part_ref,
            dst_ref=parts.at[k],
            send_sem=send.at[k],
            recv_sem=recv.at[k],
            device_id={"col": lax.rem(me + k, n)},
            device_id_type=MESH,
        )

    for k in range(1, n):
        copy(k).start()
    total = part_ref[...]
    for k in range(1, n):
        copy(k).wait_recv()
    for k in range(1, n):
        total = total + parts[k]
    lane = lax.broadcasted_iota(jnp.int32, (H, W), 1)
    mine = jnp.sum(jnp.where(lane == zone_ref[0], total, 0.0), axis=1, keepdims=True)
    mean = mine[0:1] / jnp.maximum(mine[1:2], 1.0)
    score_ref[...] = energy_ref[...] / (mean + 0.01)
    for k in range(1, n):
        copy(k).wait_send()


def score_of(zone, energy, part, n):
    vmem = pl.BlockSpec(memory_space=pltpu.VMEM)
    return pl.pallas_call(
        functools.partial(score_kernel, n),
        out_shape=jax.ShapeDtypeStruct((H, W), jnp.float32),
        in_specs=[pl.BlockSpec(memory_space=pltpu.SMEM), vmem, vmem],
        out_specs=vmem,
        scratch_shapes=[
            pltpu.VMEM((n, H, W), jnp.float32),
            pltpu.SemaphoreType.DMA((n,)),
            pltpu.SemaphoreType.DMA((n,)),
        ],
        compiler_params=pltpu.CompilerParams(collective_id=1, has_side_effects=True),
    )(zone, energy, part)


def body(n, features, zone_ids, golden_owner, defect_mask, kernels):
    tile = features[0].reshape(H * W, C).T
    kernels_t = jnp.swapaxes(kernels, 1, 2)
    golden = gather_golden(zone_ids, golden_owner, tile, n)
    energy, part = inspect(zone_ids, tile, golden, defect_mask[0], kernels_t)
    return score_of(zone_ids, energy, part, n)[None]


def solution(mesh):
    in_specs = (
        P(("groups", "col"), None, None),
        P(("groups", "col")),
        P("groups"),
        P(("groups", "col"), None, None),
        P(),
    )
    out_specs = P(("groups", "col"), None, None)
    run = functools.partial(body, mesh.shape["col"])
    return jax.shard_map(run, mesh=mesh, in_specs=in_specs, out_specs=out_specs, check_vma=False)
```

```python
import functools

import jax
import jax.numpy as jnp
from jax import lax
from jax.experimental import pallas as pl
from jax.experimental.pallas import tpu as pltpu
from jax.sharding import PartitionSpec as P

C = 64
H = 8
W = 128
SHIFT = 6
REACH = 2
Z = 8
PARTS = 2
MESH = pl.DeviceIdType.MESH


def lane_box(v):
    lane = lax.broadcasted_iota(jnp.int32, v.shape, v.ndim - 1)
    total = v
    for d in range(1, REACH + 1):
        right = pltpu.roll(v, d, v.ndim - 1)
        left = pltpu.roll(v, W - d, v.ndim - 1)
        total = total + jnp.where(lane >= d, right, 0.0) + jnp.where(lane < W - d, left, 0.0)
    return total


def rotate_rows(v, bits, sign):
    for k in range(4):
        step = 1 << k
        moved = pltpu.roll(v, (16 - step) if sign < 0 else step, v.ndim - 2)
        v = jnp.where(bits[k], moved, v)
    return v


def conv_taps(tile_f, stack, weights):
    lane = lax.rem(lax.broadcasted_iota(jnp.int32, (C, H * W), 1), W)
    pixels = H * W
    left = jnp.where(lane >= 1, pltpu.roll(tile_f, 1, 1), 0.0).astype(jnp.bfloat16)
    right = jnp.where(lane < W - 1, pltpu.roll(tile_f, pixels - 1, 1), 0.0).astype(jnp.bfloat16)
    views = (left, tile_f.astype(jnp.bfloat16), right)
    zeros = jnp.zeros((C, W), jnp.bfloat16)
    for tap in range(9):
        dy = tap // 3 - 1
        v = views[tap % 3]
        rows = slice(tap * C, (tap + 1) * C)
        if dy == 0:
            stack[rows, :] = v
        elif dy < 0:
            stack[rows, 0:W] = zeros
            stack[rows, W:pixels] = v[:, 0 : pixels - W]
        else:
            stack[rows, 0 : pixels - W] = v[:, W:pixels]
            stack[rows, pixels - W : pixels] = zeros
    return jnp.dot(weights, stack[...], preferred_element_type=jnp.float32)


def to_pixels(pieces, rows, pixels):
    wide = pieces[0].shape[1] // 128
    for k in range(PARTS):
        for j in range(wide):
            at = (k * wide + j) * H
            rows[at : at + H, :] = pieces[k][:, j * 128 : (j + 1) * 128].astype(jnp.float32)
    pairs = W * C // 128
    for y in range(H):
        v = rows[pl.ds(y, pairs, stride=H), :]
        pixels[pl.ds(y * W, pairs, stride=2), :] = v
        pixels[pl.ds(y * W + 1, pairs, stride=2), :] = pltpu.roll(v, C, 1)
    return pixels[:, 0:C]


def whole_kernel(
    n, nz, ny,
    zone_ref, owner_ref, feat_ref, mask_ref, k_ref, score_ref,
    slots, rows, pixels, t_ref, kt_ref, cross, res, stack, part, parts,
    own_sem, recv, sends, part_send, part_recv,
):
    me = lax.axis_index("col")
    core = lax.rem(me, 2)
    yy = lax.rem(me // 2, ny)
    zz = me // (2 * ny)

    def idx(z, y, c):
        return (z * ny + y) * 2 + c

    up = idx(zz + 1, yy, core)
    down = idx(zz - 1, yy, core)
    side = idx(zz, 1 - yy, core)
    mate = idx(zz, yy, 1 - core)
    has_up = zz + 1 < nz
    has_down = zz > 0

    barrier = pltpu.get_barrier_semaphore()

    def greet(dev):
        pl.semaphore_signal(barrier, inc=1, device_id={"col": dev}, device_id_type=MESH)

    @pl.when(has_up)
    def _():
        greet(up)

    @pl.when(has_down)
    def _():
        greet(down)

    if ny == 2:
        greet(side)
    greet(mate)
    peers = ny + jnp.where(has_up, 1, 0) + jnp.where(has_down, 1, 0)
    pl.semaphore_wait(barrier, peers)

    span = feat_ref.shape[2] // PARTS

    def copy(kind, slot, k, dev, own=False):
        return pltpu.make_async_remote_copy(
            src_ref=feat_ref.at[0, :, pl.ds(k * span, span)] if own else slots.at[slot, k],
            dst_ref=slots.at[slot, k],
            send_sem=sends.at[kind, slot, k],
            recv_sem=recv.at[slot, k],
            device_id={"col": dev},
            device_id_type=MESH,
        )

    def arrive(slot, k):
        copy(0, slot, k, mate).wait_recv()

    def own_copy(k):
        return pltpu.make_async_copy(
            feat_ref.at[0, :, pl.ds(k * span, span)], slots.at[me, k], own_sem.at[k]
        )

    for k in range(PARTS):

        @pl.when(has_up)
        def _():
            copy(0, me, k, up, True).start()

        @pl.when(has_down)
        def _():
            copy(1, me, k, down, True).start()

        if ny == 2:
            copy(2, me, k, side, True).start()
        copy(3, me, k, mate, True).start()
        own_copy(k).start()

    test = to_pixels([feat_ref[0, :, k * span : (k + 1) * span] for k in range(PARTS)], rows, pixels)
    t_f = test.T
    t_ref[...] = t_f
    for i in range(2):
        kt_ref[i] = k_ref[i].astype(jnp.float32).T.astype(jnp.bfloat16)

    def from_side(z, k):
        slot = idx(z, 1 - yy, core)
        arrive(slot, k)
        copy(3, slot, k, mate).start()

    for s in range(1, nz + 1):
        for k in range(PARTS):
            if s < nz:

                @pl.when(zz - s >= 0)
                def _():
                    slot = idx(zz - s, yy, core)
                    arrive(slot, k)

                    @pl.when(has_up)
                    def _():
                        copy(0, slot, k, up).start()

                    if ny == 2:
                        copy(2, slot, k, side).start()
                    copy(3, slot, k, mate).start()

                @pl.when(zz + s < nz)
                def _():
                    slot = idx(zz + s, yy, core)
                    arrive(slot, k)

                    @pl.when(has_down)
                    def _():
                        copy(1, slot, k, down).start()

                    if ny == 2:
                        copy(2, slot, k, side).start()
                    copy(3, slot, k, mate).start()

            if ny == 2:
                if s == 1:
                    from_side(zz, k)
                else:

                    @pl.when(zz - (s - 1) >= 0)
                    def _():
                        from_side(zz - (s - 1), k)

                    @pl.when(zz + (s - 1) < nz)
                    def _():
                        from_side(zz + (s - 1), k)

    for z in range(nz):
        for y in range(ny):
            for k in range(PARTS):
                arrive(idx(z, y, 1 - core), k)
    for k in range(PARTS):
        own_copy(k).wait()

    chosen = slots[owner_ref[zone_ref[0]]]
    g_f = to_pixels([chosen[k] for k in range(PARTS)], rows, pixels)
    g = g_f.astype(jnp.bfloat16)
    gt = g_f.T.astype(jnp.bfloat16)
    fold_row = lax.broadcasted_iota(jnp.int32, (8, 16, W), 0) * 16 + lax.broadcasted_iota(
        jnp.int32, (8, 16, W), 1
    )
    gap = fold_row - lax.broadcasted_iota(jnp.int32, (8, 16, W), 2)
    near = jnp.logical_and(gap >= -8, gap < 8)
    near_f = jnp.where(near, 1.0, 0.0)
    near_b = near_f.astype(jnp.bfloat16)

    def bits_of(shape):
        spin = lax.broadcasted_iota(jnp.int32, shape, len(shape) - 1) + 8
        return [((spin >> k) & 1) == 1 for k in range(4)]

    bits3 = bits_of((H, 16, W))

    def band(full):
        v = full.reshape(H, 8, 16, W)
        v = jnp.sum(v * near_f[None], axis=1)
        return lane_box(rotate_rows(v, bits3, -1))

    for y in range(H):
        gram = jnp.dot(g, t_ref[:, y * W : (y + 1) * W].astype(jnp.bfloat16), preferred_element_type=jnp.float32)
        cross[y] = band(gram)
    square = jnp.sum(g_f * g_f, axis=1, keepdims=True)
    other_rows = band(jnp.broadcast_to(square, (H * W, W)))
    others = [other_rows[r] for r in range(H)]

    t_f = t_ref[...]
    own = jnp.sum(t_f * t_f, axis=0, keepdims=True)
    own_rows = [own[:, y * W : (y + 1) * W] for y in range(H)]
    row_id = lax.broadcasted_iota(jnp.int32, (16, W), 0)
    used = jnp.logical_and(row_id >= 8 - SHIFT, row_id <= 8 + SHIFT)

    for y in range(H):
        lo_y, hi_y = max(0, y - REACH), min(H - 1, y + REACH)
        self_energy = own_rows[lo_y]
        for r in range(lo_y + 1, hi_y + 1):
            self_energy = self_energy + own_rows[r]
        self_energy = jnp.broadcast_to(lane_box(self_energy), (16, W))
        denom = jnp.zeros((16, W), jnp.float32)
        picked = {}
        for a in range(-SHIFT, SHIFT + 1):
            num = None
            oth = None
            for r in range(lo_y, hi_y + 1):
                if 0 <= r + a < H:
                    num = cross[r, r + a] if num is None else num + cross[r, r + a]
                    oth = others[r + a] if oth is None else oth + others[r + a]
            if num is None:
                expo = jnp.where(used, 1.0, 0.0)
            else:
                logit = (32.0 * num) * lax.rsqrt(self_energy * oth + 1e-05)
                expo = jnp.where(used, jnp.exp(logit), 0.0)
            denom = denom + expo
            if 0 <= y + a < H:
                picked[y + a] = expo
        stacked = jnp.stack(
            [picked[r] if r in picked else jnp.zeros((16, W), jnp.float32) for r in range(H)]
        )
        stacked = rotate_rows(stacked, bits3, 1)
        high = stacked.astype(jnp.bfloat16)
        low = (stacked - high.astype(jnp.float32)).astype(jnp.bfloat16)
        wide_high = (high[:, None] * near_b[None]).reshape(H * W, W)
        wide_low = (low[:, None] * near_b[None]).reshape(H * W, W)
        numer = jnp.dot(gt, wide_high, preferred_element_type=jnp.float32) + jnp.dot(
            gt, wide_low, preferred_element_type=jnp.float32
        )
        total = jnp.sum(denom, axis=0, keepdims=True)
        aligned = numer / total
        cols = slice(y * W, (y + 1) * W)
        res[:, cols] = (t_f[:, cols] - aligned).astype(jnp.bfloat16).astype(jnp.float32)

    residual = res[...]
    hidden = jnp.maximum(conv_taps(residual, stack, kt_ref[0]), 0.0)
    hidden = hidden.astype(jnp.bfloat16).astype(jnp.float32)
    refined = residual + conv_taps(hidden, stack, kt_ref[1])
    flat = jnp.sum(refined * refined, axis=0, keepdims=True) * (1.0 / C)
    energy = jnp.concatenate([flat[:, y * W : (y + 1) * W] for y in range(H)], axis=0)
    masked = mask_ref[0].astype(jnp.float32)
    die_sum = jnp.sum(jnp.sum(energy * masked, axis=1, keepdims=True), axis=0, keepdims=True)
    die_count = jnp.sum(jnp.sum(masked, axis=1, keepdims=True), axis=0, keepdims=True)
    lane = lax.broadcasted_iota(jnp.int32, (1, W), 1)
    zone = zone_ref[0]
    at_sum = lane == zone
    at_count = lane == zone + W // 2
    mine = jnp.where(at_sum, die_sum, jnp.where(at_count, die_count, 0.0))
    part[...] = mine

    def give(k):
        return pltpu.make_async_remote_copy(
            src_ref=part,
            dst_ref=parts.at[k],
            send_sem=part_send.at[k],
            recv_sem=part_recv.at[k],
            device_id={"col": lax.rem(me + k, n)},
            device_id_type=MESH,
        )

    for k in range(1, n):
        give(k).start()

    def sent(kind, slot, k):
        copy(kind, slot, k, mate).wait_send()

    for z in range(nz):
        slot = idx(z, yy, core)
        for k in range(PARTS):

            @pl.when(jnp.logical_and(has_up, z <= zz))
            def _():
                sent(0, slot, k)

            @pl.when(jnp.logical_and(has_down, z >= zz))
            def _():
                sent(1, slot, k)

            if ny == 2:
                sent(2, slot, k)
            for y in range(ny):
                sent(3, idx(z, y, core), k)

    for k in range(1, n):
        give(k).wait_recv()
    total = mine
    for k in range(1, n):
        total = total + parts[k]
    zone_sum = jnp.sum(jnp.where(at_sum, total, 0.0), axis=1, keepdims=True)
    zone_count = jnp.sum(jnp.where(at_count, total, 0.0), axis=1, keepdims=True)
    mean = zone_sum / jnp.maximum(zone_count, 1.0)
    score_ref[0] = energy / (mean + 0.01)
    for k in range(1, n):
        give(k).wait_send()


def body(n, features, zone_ids, golden_owner, defect_mask, kernels):
    ny = 2 if n == 16 else 1
    nz = n // (2 * ny)
    vmem = pl.BlockSpec(memory_space=pltpu.VMEM)
    smem = pl.BlockSpec(memory_space=pltpu.SMEM)
    dma = pltpu.SemaphoreType.DMA
    span = W * C // PARTS
    return pl.pallas_call(
        functools.partial(whole_kernel, n, nz, ny),
        out_shape=jax.ShapeDtypeStruct((1, H, W), jnp.float32),
        in_specs=[smem, smem, vmem, vmem, vmem],
        out_specs=vmem,
        scratch_shapes=[
            pltpu.VMEM((n, PARTS, H, span), jnp.bfloat16),
            pltpu.VMEM((H * W * C // 128, 128), jnp.float32),
            pltpu.VMEM((H * W, 128), jnp.float32),
            pltpu.VMEM((C, H * W), jnp.float32),
            pltpu.VMEM((2, C, 9 * C), jnp.bfloat16),
            pltpu.VMEM((H, H, 16, W), jnp.float32),
            pltpu.VMEM((C, H * W), jnp.float32),
            pltpu.VMEM((9 * C, H * W), jnp.bfloat16),
            pltpu.VMEM((1, W), jnp.float32),
            pltpu.VMEM((n, 1, W), jnp.float32),
            dma((PARTS,)),
            dma((n, PARTS)),
            dma((4, n, PARTS)),
            dma((n,)),
            dma((n,)),
        ],
        compiler_params=pltpu.CompilerParams(collective_id=0, has_side_effects=True),
    )(zone_ids, golden_owner, features, defect_mask, kernels)


def solution(mesh):
    in_specs = (
        P(("groups", "col"), None, None),
        P(("groups", "col")),
        P("groups"),
        P(("groups", "col"), None, None),
        P(),
    )
    out_specs = P(("groups", "col"), None, None)
    run = functools.partial(body, mesh.shape["col"])
    return jax.shard_map(run, mesh=mesh, in_specs=in_specs, out_specs=out_specs, check_vma=False)
```

```python
import functools

import jax
import jax.numpy as jnp
from jax import lax
from jax.experimental import pallas as pl
from jax.experimental.pallas import tpu as pltpu
from jax.sharding import PartitionSpec as P

C = 64
H = 8
W = 128
SHIFT = 6
REACH = 2
Z = 8
PARTS = 2
MESH = pl.DeviceIdType.MESH


def lane_box(v):
    lane = lax.broadcasted_iota(jnp.int32, v.shape, v.ndim - 1)
    total = v
    for d in range(1, REACH + 1):
        right = pltpu.roll(v, d, v.ndim - 1)
        left = pltpu.roll(v, W - d, v.ndim - 1)
        total = total + jnp.where(lane >= d, right, 0.0) + jnp.where(lane < W - d, left, 0.0)
    return total


def rotate_rows(v, bits, sign):
    for k in range(4):
        step = 1 << k
        moved = pltpu.roll(v, (16 - step) if sign < 0 else step, v.ndim - 2)
        v = jnp.where(bits[k], moved, v)
    return v


def conv_taps(tile_f, stack, weights):
    lane = lax.rem(lax.broadcasted_iota(jnp.int32, (C, H * W), 1), W)
    pixels = H * W
    left = jnp.where(lane >= 1, pltpu.roll(tile_f, 1, 1), 0.0).astype(jnp.bfloat16)
    right = jnp.where(lane < W - 1, pltpu.roll(tile_f, pixels - 1, 1), 0.0).astype(jnp.bfloat16)
    views = (left, tile_f.astype(jnp.bfloat16), right)
    zeros = jnp.zeros((C, W), jnp.bfloat16)
    for tap in range(9):
        dy = tap // 3 - 1
        v = views[tap % 3]
        rows = slice(tap * C, (tap + 1) * C)
        if dy == 0:
            stack[rows, :] = v
        elif dy < 0:
            stack[rows, 0:W] = zeros
            stack[rows, W:pixels] = v[:, 0 : pixels - W]
        else:
            stack[rows, 0 : pixels - W] = v[:, W:pixels]
            stack[rows, pixels - W : pixels] = zeros
    return jnp.dot(weights, stack[...], preferred_element_type=jnp.float32)


def to_pixels(pieces, rows, pixels):
    wide = pieces[0].shape[1] // 128
    for k in range(PARTS):
        for j in range(wide):
            at = (k * wide + j) * H
            rows[at : at + H, :] = pieces[k][:, j * 128 : (j + 1) * 128].astype(jnp.float32)
    pairs = W * C // 128
    for y in range(H):
        v = rows[pl.ds(y, pairs, stride=H), :]
        pixels[pl.ds(y * W, pairs, stride=2), :] = v
        pixels[pl.ds(y * W + 1, pairs, stride=2), :] = pltpu.roll(v, C, 1)
    return pixels[:, 0:C]


def whole_kernel(
    n, nz, ny,
    zone_ref, owner_ref, feat_ref, mask_ref, k_ref, score_ref,
    slots, rows, pixels, t_ref, cross, res, stack, part, parts,
    own_sem, recv, sends, part_send, part_recv,
):
    me = lax.axis_index("col")
    core = lax.rem(me, 2)
    yy = lax.rem(me // 2, ny)
    zz = me // (2 * ny)

    def idx(z, y, c):
        return (z * ny + y) * 2 + c

    up = idx(zz + 1, yy, core)
    down = idx(zz - 1, yy, core)
    side = idx(zz, 1 - yy, core)
    mate = idx(zz, yy, 1 - core)
    has_up = zz + 1 < nz
    has_down = zz > 0

    barrier = pltpu.get_barrier_semaphore()

    def greet(dev):
        pl.semaphore_signal(barrier, inc=1, device_id={"col": dev}, device_id_type=MESH)

    @pl.when(has_up)
    def _():
        greet(up)

    @pl.when(has_down)
    def _():
        greet(down)

    if ny == 2:
        greet(side)
    greet(mate)
    peers = ny + jnp.where(has_up, 1, 0) + jnp.where(has_down, 1, 0)
    pl.semaphore_wait(barrier, peers)

    span = feat_ref.shape[2] // PARTS

    def copy(kind, slot, k, dev, own=False):
        return pltpu.make_async_remote_copy(
            src_ref=feat_ref.at[0, :, pl.ds(k * span, span)] if own else slots.at[slot, k],
            dst_ref=slots.at[slot, k],
            send_sem=sends.at[kind, slot, k],
            recv_sem=recv.at[slot, k],
            device_id={"col": dev},
            device_id_type=MESH,
        )

    def arrive(slot, k):
        copy(0, slot, k, mate).wait_recv()

    def own_copy(k):
        return pltpu.make_async_copy(
            feat_ref.at[0, :, pl.ds(k * span, span)], slots.at[me, k], own_sem.at[k]
        )

    for k in range(PARTS):

        @pl.when(has_up)
        def _():
            copy(0, me, k, up, True).start()

        @pl.when(has_down)
        def _():
            copy(1, me, k, down, True).start()

        if ny == 2:
            copy(2, me, k, side, True).start()
        copy(3, me, k, mate, True).start()
        own_copy(k).start()

    test = to_pixels([feat_ref[0, :, k * span : (k + 1) * span] for k in range(PARTS)], rows, pixels)
    t_f = test.T
    t_ref[...] = t_f

    def from_side(z, k):
        slot = idx(z, 1 - yy, core)
        arrive(slot, k)
        copy(3, slot, k, mate).start()

    for s in range(1, nz + 1):
        for k in range(PARTS):
            if s < nz:

                @pl.when(zz - s >= 0)
                def _():
                    slot = idx(zz - s, yy, core)
                    arrive(slot, k)

                    @pl.when(has_up)
                    def _():
                        copy(0, slot, k, up).start()

                    if ny == 2:
                        copy(2, slot, k, side).start()
                    copy(3, slot, k, mate).start()

                @pl.when(zz + s < nz)
                def _():
                    slot = idx(zz + s, yy, core)
                    arrive(slot, k)

                    @pl.when(has_down)
                    def _():
                        copy(1, slot, k, down).start()

                    if ny == 2:
                        copy(2, slot, k, side).start()
                    copy(3, slot, k, mate).start()

            if ny == 2:
                if s == 1:
                    from_side(zz, k)
                else:

                    @pl.when(zz - (s - 1) >= 0)
                    def _():
                        from_side(zz - (s - 1), k)

                    @pl.when(zz + (s - 1) < nz)
                    def _():
                        from_side(zz + (s - 1), k)

    for z in range(nz):
        for y in range(ny):
            for k in range(PARTS):
                arrive(idx(z, y, 1 - core), k)
    for k in range(PARTS):
        own_copy(k).wait()

    chosen = slots[owner_ref[zone_ref[0]]]
    g_f = to_pixels([chosen[k] for k in range(PARTS)], rows, pixels)
    g = g_f.astype(jnp.bfloat16)
    gt = g_f.T.astype(jnp.bfloat16)
    fold_row = lax.broadcasted_iota(jnp.int32, (8, 16, W), 0) * 16 + lax.broadcasted_iota(
        jnp.int32, (8, 16, W), 1
    )
    gap = fold_row - lax.broadcasted_iota(jnp.int32, (8, 16, W), 2)
    near = jnp.logical_and(gap >= -8, gap < 8)
    near_f = jnp.where(near, 1.0, 0.0)
    near_b = near_f.astype(jnp.bfloat16)

    def bits_of(shape):
        spin = lax.broadcasted_iota(jnp.int32, shape, len(shape) - 1) + 8
        return [((spin >> k) & 1) == 1 for k in range(4)]

    bits3 = bits_of((H, 16, W))

    def band(full):
        v = full.reshape(H, 8, 16, W)
        v = jnp.sum(v * near_f[None], axis=1)
        return lane_box(rotate_rows(v, bits3, -1))

    for y in range(H):
        gram = jnp.dot(g, t_ref[:, y * W : (y + 1) * W].astype(jnp.bfloat16), preferred_element_type=jnp.float32)
        cross[y] = band(gram)
    square = jnp.sum(g_f * g_f, axis=1, keepdims=True)
    other_rows = band(jnp.broadcast_to(square, (H * W, W)))
    others = [other_rows[r] for r in range(H)]

    t_f = t_ref[...]
    own = jnp.sum(t_f * t_f, axis=0, keepdims=True)
    own_rows = [own[:, y * W : (y + 1) * W] for y in range(H)]
    row_id = lax.broadcasted_iota(jnp.int32, (16, W), 0)
    used = jnp.logical_and(row_id >= 8 - SHIFT, row_id <= 8 + SHIFT)

    for y in range(H):
        lo_y, hi_y = max(0, y - REACH), min(H - 1, y + REACH)
        self_energy = own_rows[lo_y]
        for r in range(lo_y + 1, hi_y + 1):
            self_energy = self_energy + own_rows[r]
        self_energy = jnp.broadcast_to(lane_box(self_energy), (16, W))
        denom = jnp.zeros((16, W), jnp.float32)
        picked = {}
        for a in range(-SHIFT, SHIFT + 1):
            num = None
            oth = None
            for r in range(lo_y, hi_y + 1):
                if 0 <= r + a < H:
                    num = cross[r, r + a] if num is None else num + cross[r, r + a]
                    oth = others[r + a] if oth is None else oth + others[r + a]
            if num is None:
                expo = jnp.where(used, 1.0, 0.0)
            else:
                logit = (32.0 * num) * lax.rsqrt(self_energy * oth + 1e-05)
                expo = jnp.where(used, jnp.exp(logit), 0.0)
            denom = denom + expo
            if 0 <= y + a < H:
                picked[y + a] = expo
        stacked = jnp.stack(
            [picked[r] if r in picked else jnp.zeros((16, W), jnp.float32) for r in range(H)]
        )
        stacked = rotate_rows(stacked, bits3, 1)
        high = stacked.astype(jnp.bfloat16)
        low = (stacked - high.astype(jnp.float32)).astype(jnp.bfloat16)
        wide_high = (high[:, None] * near_b[None]).reshape(H * W, W)
        wide_low = (low[:, None] * near_b[None]).reshape(H * W, W)
        numer = jnp.dot(gt, wide_high, preferred_element_type=jnp.float32) + jnp.dot(
            gt, wide_low, preferred_element_type=jnp.float32
        )
        total = jnp.sum(denom, axis=0, keepdims=True)
        aligned = numer / total
        cols = slice(y * W, (y + 1) * W)
        res[:, cols] = (t_f[:, cols] - aligned).astype(jnp.bfloat16).astype(jnp.float32)

    residual = res[...]
    hidden = jnp.maximum(conv_taps(residual, stack, k_ref[0]), 0.0)
    hidden = hidden.astype(jnp.bfloat16).astype(jnp.float32)
    refined = residual + conv_taps(hidden, stack, k_ref[1])
    flat = jnp.sum(refined * refined, axis=0, keepdims=True) * (1.0 / C)
    energy = jnp.concatenate([flat[:, y * W : (y + 1) * W] for y in range(H)], axis=0)
    masked = mask_ref[0].astype(jnp.float32)
    die_sum = jnp.sum(jnp.sum(energy * masked, axis=1, keepdims=True), axis=0, keepdims=True)
    die_count = jnp.sum(jnp.sum(masked, axis=1, keepdims=True), axis=0, keepdims=True)
    lane = lax.broadcasted_iota(jnp.int32, (1, W), 1)
    zone = zone_ref[0]
    at_sum = lane == zone
    at_count = lane == zone + W // 2
    mine = jnp.where(at_sum, die_sum, jnp.where(at_count, die_count, 0.0))
    part[...] = mine

    def give(k):
        return pltpu.make_async_remote_copy(
            src_ref=part,
            dst_ref=parts.at[k],
            send_sem=part_send.at[k],
            recv_sem=part_recv.at[k],
            device_id={"col": lax.rem(me + k, n)},
            device_id_type=MESH,
        )

    for k in range(1, n):
        give(k).start()

    def sent(kind, slot, k):
        copy(kind, slot, k, mate).wait_send()

    for z in range(nz):
        slot = idx(z, yy, core)
        for k in range(PARTS):

            @pl.when(jnp.logical_and(has_up, z <= zz))
            def _():
                sent(0, slot, k)

            @pl.when(jnp.logical_and(has_down, z >= zz))
            def _():
                sent(1, slot, k)

            if ny == 2:
                sent(2, slot, k)
            for y in range(ny):
                sent(3, idx(z, y, core), k)

    for k in range(1, n):
        give(k).wait_recv()
    total = mine
    for k in range(1, n):
        total = total + parts[k]
    zone_sum = jnp.sum(jnp.where(at_sum, total, 0.0), axis=1, keepdims=True)
    zone_count = jnp.sum(jnp.where(at_count, total, 0.0), axis=1, keepdims=True)
    mean = zone_sum / jnp.maximum(zone_count, 1.0)
    score_ref[0] = energy / (mean + 0.01)
    for k in range(1, n):
        give(k).wait_send()


def body(n, features, zone_ids, golden_owner, defect_mask, kernels):
    ny = 2 if n == 16 else 1
    nz = n // (2 * ny)
    vmem = pl.BlockSpec(memory_space=pltpu.VMEM)
    smem = pl.BlockSpec(memory_space=pltpu.SMEM)
    dma = pltpu.SemaphoreType.DMA
    span = W * C // PARTS
    return pl.pallas_call(
        functools.partial(whole_kernel, n, nz, ny),
        out_shape=jax.ShapeDtypeStruct((1, H, W), jnp.float32),
        in_specs=[smem, smem, vmem, vmem, vmem],
        out_specs=vmem,
        scratch_shapes=[
            pltpu.VMEM((n, PARTS, H, span), jnp.bfloat16),
            pltpu.VMEM((H * W * C // 128, 128), jnp.float32),
            pltpu.VMEM((H * W, 128), jnp.float32),
            pltpu.VMEM((C, H * W), jnp.float32),
            pltpu.VMEM((H, H, 16, W), jnp.float32),
            pltpu.VMEM((C, H * W), jnp.float32),
            pltpu.VMEM((9 * C, H * W), jnp.bfloat16),
            pltpu.VMEM((1, W), jnp.float32),
            pltpu.VMEM((n, 1, W), jnp.float32),
            dma((PARTS,)),
            dma((n, PARTS)),
            dma((4, n, PARTS)),
            dma((n,)),
            dma((n,)),
        ],
        compiler_params=pltpu.CompilerParams(collective_id=0, has_side_effects=True),
    )(zone_ids, golden_owner, features, defect_mask, jnp.swapaxes(kernels, 1, 2))


def solution(mesh):
    in_specs = (
        P(("groups", "col"), None, None),
        P(("groups", "col")),
        P("groups"),
        P(("groups", "col"), None, None),
        P(),
    )
    out_specs = P(("groups", "col"), None, None)
    run = functools.partial(body, mesh.shape["col"])
    return jax.shard_map(run, mesh=mesh, in_specs=in_specs, out_specs=out_specs, check_vma=False)
```

```python
import functools

import jax
import jax.numpy as jnp
from jax import lax
from jax.experimental import pallas as pl
from jax.experimental.pallas import tpu as pltpu
from jax.sharding import PartitionSpec as P

C = 64
H = 8
W = 128
SHIFT = 6
REACH = 2
Z = 8
PARTS = 1
MESH = pl.DeviceIdType.MESH


def lane_box(v):
    lane = lax.broadcasted_iota(jnp.int32, v.shape, v.ndim - 1)
    total = v
    for d in range(1, REACH + 1):
        right = pltpu.roll(v, d, v.ndim - 1)
        left = pltpu.roll(v, W - d, v.ndim - 1)
        total = total + jnp.where(lane >= d, right, 0.0) + jnp.where(lane < W - d, left, 0.0)
    return total


def rotate_rows(v, bits, sign):
    for k in range(4):
        step = 1 << k
        moved = pltpu.roll(v, (16 - step) if sign < 0 else step, v.ndim - 2)
        v = jnp.where(bits[k], moved, v)
    return v


def conv_taps(tile_f, stack, weights):
    lane = lax.rem(lax.broadcasted_iota(jnp.int32, (C, H * W), 1), W)
    pixels = H * W
    left = jnp.where(lane >= 1, pltpu.roll(tile_f, 1, 1), 0.0).astype(jnp.bfloat16)
    right = jnp.where(lane < W - 1, pltpu.roll(tile_f, pixels - 1, 1), 0.0).astype(jnp.bfloat16)
    views = (left, tile_f.astype(jnp.bfloat16), right)
    zeros = jnp.zeros((C, W), jnp.bfloat16)
    for tap in range(9):
        dy = tap // 3 - 1
        v = views[tap % 3]
        rows = slice(tap * C, (tap + 1) * C)
        if dy == 0:
            stack[rows, :] = v
        elif dy < 0:
            stack[rows, 0:W] = zeros
            stack[rows, W:pixels] = v[:, 0 : pixels - W]
        else:
            stack[rows, 0 : pixels - W] = v[:, W:pixels]
            stack[rows, pixels - W : pixels] = zeros
    return jnp.dot(weights, stack[...], preferred_element_type=jnp.float32)


def to_pixels(pieces, rows, pixels):
    wide = pieces[0].shape[1] // 128
    for k in range(PARTS):
        for j in range(wide):
            at = (k * wide + j) * H
            rows[at : at + H, :] = pieces[k][:, j * 128 : (j + 1) * 128].astype(jnp.float32)
    pairs = W * C // 128
    for y in range(H):
        v = rows[pl.ds(y, pairs, stride=H), :]
        pixels[pl.ds(y * W, pairs, stride=2), :] = v
        pixels[pl.ds(y * W + 1, pairs, stride=2), :] = pltpu.roll(v, C, 1)
    return pixels[:, 0:C]


def whole_kernel(
    n, nz, ny,
    zone_ref, owner_ref, feat_ref, mask_ref, k_ref, score_ref,
    slots, rows, pixels, t_ref, cross, res, stack, part, parts,
    own_sem, recv, sends, part_send, part_recv,
):
    me = lax.axis_index("col")
    core = lax.rem(me, 2)
    yy = lax.rem(me // 2, ny)
    zz = me // (2 * ny)

    def idx(z, y, c):
        return (z * ny + y) * 2 + c

    up = idx(zz + 1, yy, core)
    down = idx(zz - 1, yy, core)
    side = idx(zz, 1 - yy, core)
    mate = idx(zz, yy, 1 - core)
    has_up = zz + 1 < nz
    has_down = zz > 0

    barrier = pltpu.get_barrier_semaphore()

    def greet(dev):
        pl.semaphore_signal(barrier, inc=1, device_id={"col": dev}, device_id_type=MESH)

    @pl.when(has_up)
    def _():
        greet(up)

    @pl.when(has_down)
    def _():
        greet(down)

    if ny == 2:
        greet(side)
    greet(mate)
    peers = ny + jnp.where(has_up, 1, 0) + jnp.where(has_down, 1, 0)
    pl.semaphore_wait(barrier, peers)

    span = feat_ref.shape[2] // PARTS

    def copy(kind, slot, k, dev, own=False):
        return pltpu.make_async_remote_copy(
            src_ref=feat_ref.at[0, :, pl.ds(k * span, span)] if own else slots.at[slot, k],
            dst_ref=slots.at[slot, k],
            send_sem=sends.at[kind, slot, k],
            recv_sem=recv.at[slot, k],
            device_id={"col": dev},
            device_id_type=MESH,
        )

    def arrive(slot, k):
        copy(0, slot, k, mate).wait_recv()

    def own_copy(k):
        return pltpu.make_async_copy(
            feat_ref.at[0, :, pl.ds(k * span, span)], slots.at[me, k], own_sem.at[k]
        )

    for k in range(PARTS):

        @pl.when(has_up)
        def _():
            copy(0, me, k, up, True).start()

        @pl.when(has_down)
        def _():
            copy(1, me, k, down, True).start()

        if ny == 2:
            copy(2, me, k, side, True).start()
        copy(3, me, k, mate, True).start()
        own_copy(k).start()

    test = to_pixels([feat_ref[0, :, k * span : (k + 1) * span] for k in range(PARTS)], rows, pixels)
    t_f = test.T
    t_ref[...] = t_f

    def from_side(z, k):
        slot = idx(z, 1 - yy, core)
        arrive(slot, k)
        copy(3, slot, k, mate).start()

    for s in range(1, nz + 1):
        for k in range(PARTS):
            if s < nz:

                @pl.when(zz - s >= 0)
                def _():
                    slot = idx(zz - s, yy, core)
                    arrive(slot, k)

                    @pl.when(has_up)
                    def _():
                        copy(0, slot, k, up).start()

                    if ny == 2:
                        copy(2, slot, k, side).start()
                    copy(3, slot, k, mate).start()

                @pl.when(zz + s < nz)
                def _():
                    slot = idx(zz + s, yy, core)
                    arrive(slot, k)

                    @pl.when(has_down)
                    def _():
                        copy(1, slot, k, down).start()

                    if ny == 2:
                        copy(2, slot, k, side).start()
                    copy(3, slot, k, mate).start()

            if ny == 2:
                if s == 1:
                    from_side(zz, k)
                else:

                    @pl.when(zz - (s - 1) >= 0)
                    def _():
                        from_side(zz - (s - 1), k)

                    @pl.when(zz + (s - 1) < nz)
                    def _():
                        from_side(zz + (s - 1), k)

    for z in range(nz):
        for y in range(ny):
            for k in range(PARTS):
                arrive(idx(z, y, 1 - core), k)
    for k in range(PARTS):
        own_copy(k).wait()

    chosen = slots[owner_ref[zone_ref[0]]]
    g_f = to_pixels([chosen[k] for k in range(PARTS)], rows, pixels)
    g = g_f.astype(jnp.bfloat16)
    gt = g_f.T.astype(jnp.bfloat16)
    fold_row = lax.broadcasted_iota(jnp.int32, (8, 16, W), 0) * 16 + lax.broadcasted_iota(
        jnp.int32, (8, 16, W), 1
    )
    gap = fold_row - lax.broadcasted_iota(jnp.int32, (8, 16, W), 2)
    near = jnp.logical_and(gap >= -8, gap < 8)
    near_f = jnp.where(near, 1.0, 0.0)
    near_b = near_f.astype(jnp.bfloat16)

    def bits_of(shape):
        spin = lax.broadcasted_iota(jnp.int32, shape, len(shape) - 1) + 8
        return [((spin >> k) & 1) == 1 for k in range(4)]

    bits3 = bits_of((H, 16, W))

    def band(full):
        v = full.reshape(H, 8, 16, W)
        v = jnp.sum(v * near_f[None], axis=1)
        return lane_box(rotate_rows(v, bits3, -1))

    for y in range(H):
        gram = jnp.dot(g, t_ref[:, y * W : (y + 1) * W].astype(jnp.bfloat16), preferred_element_type=jnp.float32)
        cross[y] = band(gram)
    square = jnp.sum(g_f * g_f, axis=1, keepdims=True)
    other_rows = band(jnp.broadcast_to(square, (H * W, W)))
    others = [other_rows[r] for r in range(H)]

    t_f = t_ref[...]
    own = jnp.sum(t_f * t_f, axis=0, keepdims=True)
    own_rows = [own[:, y * W : (y + 1) * W] for y in range(H)]
    row_id = lax.broadcasted_iota(jnp.int32, (16, W), 0)
    used = jnp.logical_and(row_id >= 8 - SHIFT, row_id <= 8 + SHIFT)

    for y in range(H):
        lo_y, hi_y = max(0, y - REACH), min(H - 1, y + REACH)
        self_energy = own_rows[lo_y]
        for r in range(lo_y + 1, hi_y + 1):
            self_energy = self_energy + own_rows[r]
        self_energy = jnp.broadcast_to(lane_box(self_energy), (16, W))
        denom = jnp.zeros((16, W), jnp.float32)
        picked = {}
        for a in range(-SHIFT, SHIFT + 1):
            num = None
            oth = None
            for r in range(lo_y, hi_y + 1):
                if 0 <= r + a < H:
                    num = cross[r, r + a] if num is None else num + cross[r, r + a]
                    oth = others[r + a] if oth is None else oth + others[r + a]
            if num is None:
                expo = jnp.where(used, 1.0, 0.0)
            else:
                logit = (32.0 * num) * lax.rsqrt(self_energy * oth + 1e-05)
                expo = jnp.where(used, jnp.exp(logit), 0.0)
            denom = denom + expo
            if 0 <= y + a < H:
                picked[y + a] = expo
        stacked = jnp.stack(
            [picked[r] if r in picked else jnp.zeros((16, W), jnp.float32) for r in range(H)]
        )
        stacked = rotate_rows(stacked, bits3, 1)
        high = stacked.astype(jnp.bfloat16)
        low = (stacked - high.astype(jnp.float32)).astype(jnp.bfloat16)
        wide_high = (high[:, None] * near_b[None]).reshape(H * W, W)
        wide_low = (low[:, None] * near_b[None]).reshape(H * W, W)
        numer = jnp.dot(gt, wide_high, preferred_element_type=jnp.float32) + jnp.dot(
            gt, wide_low, preferred_element_type=jnp.float32
        )
        total = jnp.sum(denom, axis=0, keepdims=True)
        aligned = numer / total
        cols = slice(y * W, (y + 1) * W)
        res[:, cols] = (t_f[:, cols] - aligned).astype(jnp.bfloat16).astype(jnp.float32)

    residual = res[...]
    hidden = jnp.maximum(conv_taps(residual, stack, k_ref[0]), 0.0)
    hidden = hidden.astype(jnp.bfloat16).astype(jnp.float32)
    refined = residual + conv_taps(hidden, stack, k_ref[1])
    flat = jnp.sum(refined * refined, axis=0, keepdims=True) * (1.0 / C)
    energy = jnp.concatenate([flat[:, y * W : (y + 1) * W] for y in range(H)], axis=0)
    masked = mask_ref[0].astype(jnp.float32)
    die_sum = jnp.sum(jnp.sum(energy * masked, axis=1, keepdims=True), axis=0, keepdims=True)
    die_count = jnp.sum(jnp.sum(masked, axis=1, keepdims=True), axis=0, keepdims=True)
    lane = lax.broadcasted_iota(jnp.int32, (1, W), 1)
    zone = zone_ref[0]
    at_sum = lane == zone
    at_count = lane == zone + W // 2
    mine = jnp.where(at_sum, die_sum, jnp.where(at_count, die_count, 0.0))
    part[...] = mine

    def give(k):
        return pltpu.make_async_remote_copy(
            src_ref=part,
            dst_ref=parts.at[k],
            send_sem=part_send.at[k],
            recv_sem=part_recv.at[k],
            device_id={"col": lax.rem(me + k, n)},
            device_id_type=MESH,
        )

    for k in range(1, n):
        give(k).start()

    def sent(kind, slot, k):
        copy(kind, slot, k, mate).wait_send()

    for z in range(nz):
        slot = idx(z, yy, core)
        for k in range(PARTS):

            @pl.when(jnp.logical_and(has_up, z <= zz))
            def _():
                sent(0, slot, k)

            @pl.when(jnp.logical_and(has_down, z >= zz))
            def _():
                sent(1, slot, k)

            if ny == 2:
                sent(2, slot, k)
            for y in range(ny):
                sent(3, idx(z, y, core), k)

    for k in range(1, n):
        give(k).wait_recv()
    total = mine
    for k in range(1, n):
        total = total + parts[k]
    zone_sum = jnp.sum(jnp.where(at_sum, total, 0.0), axis=1, keepdims=True)
    zone_count = jnp.sum(jnp.where(at_count, total, 0.0), axis=1, keepdims=True)
    mean = zone_sum / jnp.maximum(zone_count, 1.0)
    score_ref[0] = energy / (mean + 0.01)
    for k in range(1, n):
        give(k).wait_send()


def body(n, features, zone_ids, golden_owner, defect_mask, kernels):
    ny = 2 if n == 16 else 1
    nz = n // (2 * ny)
    vmem = pl.BlockSpec(memory_space=pltpu.VMEM)
    smem = pl.BlockSpec(memory_space=pltpu.SMEM)
    dma = pltpu.SemaphoreType.DMA
    span = W * C // PARTS
    return pl.pallas_call(
        functools.partial(whole_kernel, n, nz, ny),
        out_shape=jax.ShapeDtypeStruct((1, H, W), jnp.float32),
        in_specs=[smem, smem, vmem, vmem, vmem],
        out_specs=vmem,
        scratch_shapes=[
            pltpu.VMEM((n, PARTS, H, span), jnp.bfloat16),
            pltpu.VMEM((H * W * C // 128, 128), jnp.float32),
            pltpu.VMEM((H * W, 128), jnp.float32),
            pltpu.VMEM((C, H * W), jnp.float32),
            pltpu.VMEM((H, H, 16, W), jnp.float32),
            pltpu.VMEM((C, H * W), jnp.float32),
            pltpu.VMEM((9 * C, H * W), jnp.bfloat16),
            pltpu.VMEM((1, W), jnp.float32),
            pltpu.VMEM((n, 1, W), jnp.float32),
            dma((PARTS,)),
            dma((n, PARTS)),
            dma((4, n, PARTS)),
            dma((n,)),
            dma((n,)),
        ],
        compiler_params=pltpu.CompilerParams(collective_id=0, has_side_effects=True),
    )(zone_ids, golden_owner, features, defect_mask, jnp.swapaxes(kernels, 1, 2))


def solution(mesh):
    in_specs = (
        P(("groups", "col"), None, None),
        P(("groups", "col")),
        P("groups"),
        P(("groups", "col"), None, None),
        P(),
    )
    out_specs = P(("groups", "col"), None, None)
    run = functools.partial(body, mesh.shape["col"])
    return jax.shard_map(run, mesh=mesh, in_specs=in_specs, out_specs=out_specs, check_vma=False)
```
